32 devices in a mesh: blk: 8 (over y, x, core), fsdp: 4 (over z).
Axes of the slice: x: 2, y: 2, z: 4, core: 2. Of those that a mesh axis runs over, the one named last changes fastest.
Arguments:
- x_forward: bfloat16 [8192, 4096], P(('blk', 'fsdp'))
- seg_forward: int32 [32, 256], P(('blk', 'fsdp')), may hold values from 0 to 3, never falling along the last dimension, each value on 1 to 128 neighbouring positions
- x_saved: bfloat16 [8192, 4096], P(('blk', 'fsdp'))
- x_earlier: bfloat16 [8192, 4096], P(('blk', 'fsdp'))
- cotangent: bfloat16 [8192, 4096], P(('blk', 'fsdp')), may hold values from -0.119628906 to 0.119628906
- seg_backward: int32 [32, 256], P(('blk', 'fsdp')), may hold values from 0 to 3, never falling along the last dimension, each value on 1 to 128 neighbouring positions
- gain: bfloat16 [8, 4096], P('blk', 'fsdp'), may hold values from 0.25 to 1.75
- qkv: bfloat16 [8, 4096, 768], P('blk', 'fsdp')
- proj: bfloat16 [8, 512, 4096], P('blk', None, 'fsdp'), may hold values from -0.25 to 0.25
- sum_gain: float32 [8, 4096], P('blk', 'fsdp'), may hold values from -6 to 6
- sum_qkv: float32 [8, 4096, 768], P('blk', 'fsdp'), may hold values from -6 to 6
- sum_proj: float32 [8, 512, 4096], P('blk', None, 'fsdp'), may hold values from -6 to 6
Outputs:
- hidden_out: bfloat16 [8192, 4096], P(('blk', 'fsdp'))
- new_sum_gain: float32 [8, 4096], P('blk', 'fsdp')
- new_sum_qkv: float32 [8, 4096, 768], P('blk', 'fsdp')
- new_sum_proj: float32 [8, 512, 4096], P('blk', None, 'fsdp')
The draws below stay inside these ranges and needn't reach their ends.
Inputs may be any that keep to these rules, and one draw needn't show every extreme that they name: `seg_forward`: each row of ids never falls along the micro-batch. `seg_backward`: each row of ids never falls along the micro-batch.
All inputs are finite; a program needn't handle non-finite values.
Results may differ from the reference program's by a relative error of at most 0.018.
The reference program's roundings to bfloat16 on the way count: a program that leaves them out, or rounds other values in their place, can miss the bound.
Values may be sent and summed in bfloat16 or wider, within the bound.
No kernel may reach another device: no remote copies, remote signals or barrier semaphores. Data moves between devices by JAX's collectives and lax.ppermute only.
A program may use at most 192 MiB of HBM per device.

```python
import math
import jax
import jax.numpy as jnp
import numpy as np
from jax import lax

D = 4096
HEADS = 4
HEAD_DIM = 128
TOK_DEV = 256
SEGS = 4
QKV = 768
ATT = 512
MICRO = 32
TOKENS = 8192
N_BLK = 8
N_FSDP = 4


def scaled_rows(key, row_count, col_count):
    base_key, row_key, col_key = jax.random.split(key, 3)
    base_draw = jax.random.normal(base_key, (row_count, col_count), jnp.float32)
    row_scale = jnp.exp(jax.random.uniform(row_key, (row_count, 1), jnp.float32, math.log(0.3), math.log(3.0)))
    col_scale = jnp.exp(jax.random.uniform(col_key, (1, col_count), jnp.float32, math.log(0.3), math.log(3.0)))
    return (base_draw * row_scale * col_scale).astype(jnp.bfloat16)


def projection_draw(key):
    weight_key = jax.random.fold_in(key, 0)
    weights = jax.random.normal(weight_key, (N_BLK, D, QKV), jnp.float32) * D ** (-0.5)
    return weights.astype(jnp.bfloat16)


def draw_x_forward(key, part):
    return scaled_rows(jax.random.fold_in(key, 11), TOKENS, D)


def draw_x_saved(key, part):
    return scaled_rows(jax.random.fold_in(key, 13), TOKENS, D)


def draw_x_earlier(key, part):
    return scaled_rows(jax.random.fold_in(key, 17), TOKENS, D)


def draw_qkv(key, part):
    return projection_draw(jax.random.fold_in(key, 31))


def steps_of(rng, dims, cuts, low, top_value):
    def one(dim, parts):
        heights = jax.random.uniform(jax.random.fold_in(jax.random.fold_in(rng, 6), dim), (parts,), jnp.float32, low / len(cuts), top_value / len(cuts))
        return jnp.repeat(jnp.exp(heights), dims[dim] // parts).reshape((-1,) + (1,) * (len(dims) - dim - 1))

    level = one(*cuts[0])
    for cut in cuts[1:]:
        level = level * one(*cut)
    return level


def profile(number_of, total, limit, lean):
    weights = [(1 << 20) // math.isqrt(standing ** lean) + 1 for standing in range(2, number_of + 1)]
    surplus, given = total - limit - (number_of - 1), [1] * (number_of - 1)
    while surplus > 0:
        movable = [i for i in range(number_of - 1) if given[i] < limit]
        whole, remaining = sum([weights[i] for i in movable]), surplus
        for i in movable:
            extra = min(limit - given[i], max(1, remaining * weights[i] // whole), surplus)
            given[i] = given[i] + extra
            surplus = surplus - extra
    return np.array([limit] + given)


def ragged(stream_key, count, total, limit, skew):
    if count == 2:
        one = jax.random.randint(stream_key, (), max(1, total - limit), min(limit, total - 1) + 1)
        return jnp.stack([one, total - one])
    lengths = jnp.asarray(profile(count, total, limit, skew), jnp.int32)
    couples = (count - 1) // 2
    source_of, sink = lengths[1:1 + 2 * couples:2], lengths[2:2 + 2 * couples:2]
    room = jnp.minimum(source_of - 1, limit - sink)
    shifted = jax.random.randint(jax.random.fold_in(stream_key, 1), (couples,), 0, 1 << 20) % (room + 1)
    lengths = lengths.at[1:1 + 2 * couples:2].set(source_of - shifted).at[2:2 + 2 * couples:2].set(sink + shifted)
    return lengths[jax.random.permutation(jax.random.fold_in(stream_key, 2), count)]


def bell_draw(key, dims, deviation, bound, cuts=(), held_as=jnp.bfloat16):
    loudness = steps_of(key, dims, cuts, -0.22, 0.18) if cuts else 1.0
    entries = jax.random.normal(key, dims, jnp.float32) * deviation * loudness
    return jnp.minimum(jnp.maximum(entries, -bound), bound).astype(held_as)


def setup_inputs(seed: int = 0) -> dict:
    seeds = jax.random.split(jax.random.key(seed), 13)
    return {
        "x_forward": draw_x_forward(jax.random.fold_in(seeds[12], 71), 0),
        "seg_forward": jax.vmap(lambda own: jnp.searchsorted(jnp.cumsum(ragged(own, SEGS, TOK_DEV, TOK_DEV // 2, 0)), jnp.arange(TOK_DEV), side="right"))(jax.random.split(seeds[1], MICRO)).reshape((MICRO, TOK_DEV)).astype(jnp.int32),
        "x_saved": draw_x_saved(jax.random.fold_in(seeds[12], 71), 0),
        "x_earlier": draw_x_earlier(jax.random.fold_in(seeds[12], 71), 0),
        "cotangent": bell_draw(seeds[4], (TOKENS, D), 0.02, 0.119628906, ((0, 32),)),
        "seg_backward": jax.vmap(lambda own: jnp.searchsorted(jnp.cumsum(ragged(own, SEGS, TOK_DEV, TOK_DEV // 2, 0)), jnp.arange(TOK_DEV), side="right"))(jax.random.split(seeds[5], MICRO)).reshape((MICRO, TOK_DEV)).astype(jnp.int32),
        "gain": jnp.clip(1.0 + 0.15 * jax.random.normal(seeds[6], (N_BLK, D), jnp.float32), 0.25, 1.75).astype(jnp.bfloat16),
        "qkv": draw_qkv(jax.random.fold_in(seeds[12], 71), 0),
        "proj": bell_draw(seeds[8], (N_BLK, ATT, D), ATT ** -0.5, 0.25, ((0, 8), (2, 4))),
        "sum_gain": bell_draw(seeds[9], (N_BLK, D), 1.0, 6.0, ((0, 8), (1, 4)), jnp.float32),
        "sum_qkv": bell_draw(seeds[10], (N_BLK, D, QKV), 1.0, 6.0, ((0, 8), (1, 4)), jnp.float32),
        "sum_proj": bell_draw(seeds[11], (N_BLK, ATT, D), 1.0, 6.0, ((0, 8), (2, 4)), jnp.float32),
    }


def attention_mask(segments):
    count = segments.shape[0]
    row_ids = lax.broadcasted_iota(jnp.int32, (count, count), 0)
    col_ids = lax.broadcasted_iota(jnp.int32, (count, count), 1)
    return (col_ids <= row_ids) & (segments[:, None] == segments[None, :])

def layer_parts(tokens, segments, norm_gain, qkv_weight):
    count = tokens.shape[0]
    att_width = HEADS * HEAD_DIM
    wide_rows = tokens.astype(jnp.float32)
    inv_rms = lax.rsqrt(lax.optimization_barrier(jnp.mean(wide_rows * wide_rows, axis=1, keepdims=True)) + 1e-05)
    normed = (wide_rows * inv_rms * norm_gain.astype(jnp.float32)[None, :]).astype(jnp.bfloat16)
    projected = jnp.dot(normed, qkv_weight, preferred_element_type=jnp.float32).astype(jnp.bfloat16)
    queries = projected[:, :att_width].reshape(count, HEADS, HEAD_DIM)
    key_rows = projected[:, att_width:att_width + HEAD_DIM]
    values = projected[:, att_width + HEAD_DIM:]
    score_scale = HEAD_DIM ** (-0.5)
    scores = jnp.einsum('thd,sd->hts', queries.astype(jnp.float32), key_rows.astype(jnp.float32)) * score_scale
    allowed = attention_mask(segments)[None]
    scores = jnp.where(allowed, scores, -1e+30)
    row_max = lax.optimization_barrier(jnp.max(scores, axis=2, keepdims=True))
    expo = jnp.where(allowed, jnp.exp(scores - row_max), 0.0)
    attn_probs = expo / lax.optimization_barrier(jnp.sum(expo, axis=2, keepdims=True))
    attn_low = attn_probs.astype(jnp.bfloat16)
    attended = jnp.einsum('hts,sd->thd', attn_low.astype(jnp.float32), values.astype(jnp.float32))
    attended = attended.reshape(count, att_width).astype(jnp.bfloat16)
    return (wide_rows, inv_rms, normed, queries, key_rows, values, attn_probs, attn_low, attended)

def layer_forward(tokens, segments, layer_weights):
    norm_gain, qkv_weight, proj_weight = layer_weights
    pieces_all = layer_parts(tokens, segments, norm_gain, qkv_weight)
    branch_out = jnp.dot(pieces_all[8], proj_weight, preferred_element_type=jnp.float32)
    return (pieces_all[0] + branch_out).astype(jnp.bfloat16)

def layer_backward(tokens, segments, layer_weights, upstream, with_input):
    norm_gain, qkv_weight, proj_weight = layer_weights
    wide_rows, inv_rms, normed, queries, key_rows, values, attn_probs, attn_low, attended = layer_parts(tokens, segments, norm_gain, qkv_weight)
    count = tokens.shape[0]
    d_att = lax.dot_general(upstream, proj_weight, (((1,), (1,)), ((), ())), preferred_element_type=jnp.float32).astype(jnp.bfloat16)
    grad_proj = lax.dot_general(attended, upstream, (((0,), (0,)), ((), ())), preferred_element_type=jnp.float32)
    d_heads = d_att.reshape(count, HEADS, HEAD_DIM).astype(jnp.float32)
    d_probs = jnp.einsum('thd,sd->hts', d_heads, values.astype(jnp.float32))
    grad_values = jnp.einsum('hts,thd->sd', attn_low.astype(jnp.float32), d_heads)
    row_inner = lax.optimization_barrier(jnp.sum(d_probs * attn_probs, axis=2, keepdims=True))
    d_scores = (attn_probs * (d_probs - row_inner) * HEAD_DIM ** (-0.5)).astype(jnp.bfloat16)
    grad_queries = jnp.einsum('hts,sd->thd', d_scores.astype(jnp.float32), key_rows.astype(jnp.float32)).reshape(count, HEADS * HEAD_DIM)
    grad_keys = jnp.einsum('hts,thd->sd', d_scores.astype(jnp.float32), queries.astype(jnp.float32))
    d_projected = jnp.concatenate([grad_queries, grad_keys, grad_values], axis=1).astype(jnp.bfloat16)
    grad_qkv = lax.dot_general(normed, d_projected, (((0,), (0,)), ((), ())), preferred_element_type=jnp.float32)
    d_normed = lax.dot_general(d_projected, qkv_weight, (((1,), (1,)), ((), ())), preferred_element_type=jnp.float32)
    grad_gain = lax.optimization_barrier(jnp.sum(d_normed * wide_rows * inv_rms, axis=0))
    grad_terms = (grad_gain, grad_qkv, grad_proj)
    if not with_input:
        return (grad_terms, upstream)
    scaled = d_normed * norm_gain.astype(jnp.float32)[None, :]
    d_wide = inv_rms * scaled - wide_rows * inv_rms ** 3 * lax.optimization_barrier(jnp.mean(scaled * wide_rows, axis=1, keepdims=True))
    d_tokens = (upstream.astype(jnp.float32) + d_wide).astype(jnp.bfloat16)
    return (grad_terms, d_tokens)

def pick_layer(stack, cycle_pos):
    return lax.dynamic_index_in_dim(stack, cycle_pos, 0, keepdims=False)

def reference(x_forward, seg_forward, x_saved, x_earlier, cotangent, seg_backward, gain, qkv, proj, sum_gain, sum_qkv, sum_proj):

    def per_shard(cycle_pos, shard_pos):
        dev_index = cycle_pos * N_FSDP + shard_pos
        start_row = dev_index * TOK_DEV
        rows_fwd = lax.dynamic_slice_in_dim(x_forward, start_row, TOK_DEV, 0)
        rows_saved = lax.dynamic_slice_in_dim(x_saved, start_row, TOK_DEV, 0)
        rows_early = lax.dynamic_slice_in_dim(x_earlier, start_row, TOK_DEV, 0)
        rows_cot = lax.dynamic_slice_in_dim(cotangent, start_row, TOK_DEV, 0)
        ids_fwd = pick_layer(seg_forward, dev_index)
        ids_bwd = pick_layer(seg_backward, dev_index)
        before_pos = (cycle_pos + N_BLK - 1) % N_BLK
        layer_now = (pick_layer(gain, cycle_pos), pick_layer(qkv, cycle_pos), pick_layer(proj, cycle_pos))
        layer_next = (pick_layer(gain, before_pos), pick_layer(qkv, before_pos), pick_layer(proj, before_pos))
        hidden = layer_forward(rows_fwd, ids_fwd, layer_now)
        result = layer_forward(hidden, ids_fwd, layer_next)
        terms_one, d_hidden = layer_backward(rows_saved, ids_bwd, layer_now, rows_cot, True)
        terms_two, unused = layer_backward(rows_early, ids_bwd, layer_next, d_hidden, False)
        return (result, tuple((term.astype(jnp.bfloat16) for term in terms_one)), tuple((term.astype(jnp.bfloat16) for term in terms_two)))

    def per_cycle(cycle_pos):
        results, terms_one, terms_two = lax.map(lambda shard_pos: per_shard(cycle_pos, shard_pos), jnp.arange(N_FSDP, dtype=jnp.int32))
        sums_one = tuple((lax.optimization_barrier(jnp.sum(term.astype(jnp.float32), axis=0)) for term in terms_one))
        sums_two = tuple((lax.optimization_barrier(jnp.sum(term.astype(jnp.float32), axis=0)) for term in terms_two))
        return (results, sums_one, sums_two)
    results, sums_one, sums_two = lax.map(per_cycle, jnp.arange(N_BLK, dtype=jnp.int32))
    hidden_out = results.reshape(N_BLK * N_FSDP * TOK_DEV, D)
    new_sum_gain = jnp.roll(sum_gain + sums_one[0], 1, axis=0) + sums_two[0]
    new_sum_qkv = jnp.roll(sum_qkv + sums_one[1], 1, axis=0) + sums_two[1]
    new_sum_proj = jnp.roll(sum_proj + sums_one[2], 1, axis=0) + sums_two[2]
    return (hidden_out, new_sum_gain, new_sum_qkv, new_sum_proj)
```

```python
import jax
import jax.numpy as jnp
from jax import lax
from jax.experimental import pallas as pl
from jax.experimental.pallas import tpu as pltpu
from jax.sharding import PartitionSpec as P

HEADS = 4
HEAD_DIM = 128
F32 = jnp.float32
BF16 = jnp.bfloat16


def shifted(value, axis, steps):
    count = lax.axis_size(axis)
    pairs = [(source, (source + steps) % count) for source in range(count)]
    return lax.ppermute(value, axis, pairs)


def contract(a, b, dim_a, dim_b):
    return lax.dot_general(a, b, (((dim_a,), (dim_b,)), ((), ())), preferred_element_type=F32)


def attend_kernel(proj_ref, col_ref, row_ref, att_ref, prob_ref):
    count = proj_ref.shape[0]
    width = HEADS * HEAD_DIM
    rows = lax.broadcasted_iota(jnp.int32, (count, count), 0)
    cols = lax.broadcasted_iota(jnp.int32, (count, count), 1)
    allowed = (cols <= rows) & (col_ref[...] == row_ref[0])
    keys = proj_ref[:, width : width + HEAD_DIM]
    values = proj_ref[:, width + HEAD_DIM :]
    for head in range(HEADS):
        part = slice(head * HEAD_DIM, (head + 1) * HEAD_DIM)
        scores = contract(proj_ref[:, part], keys, 1, 1) * HEAD_DIM ** (-0.5)
        scores = jnp.where(allowed, scores, -1e30)
        top = jnp.max(scores, axis=1, keepdims=True)
        expo = jnp.where(allowed, jnp.exp(scores - top), 0.0)
        probs = expo / jnp.sum(expo, axis=1, keepdims=True)
        prob_ref[head] = probs
        att_ref[:, part] = contract(probs.astype(BF16), values, 1, 0).astype(BF16)


def attend(projected, ids):
    micro, count = ids.shape
    width = projected.shape[1]
    att_width = HEADS * HEAD_DIM
    return pl.pallas_call(
        attend_kernel,
        grid=(micro,),
        in_specs=[
            pl.BlockSpec((count, width), lambda m: (m, 0)),
            pl.BlockSpec((count, 1), lambda m: (m, 0)),
            pl.BlockSpec((1, 1, count), lambda m: (m, 0, 0)),
        ],
        out_specs=[
            pl.BlockSpec((count, att_width), lambda m: (m, 0)),
            pl.BlockSpec((HEADS, count, count), lambda m: (m, 0, 0)),
        ],
        out_shape=[
            jax.ShapeDtypeStruct((micro * count, att_width), BF16),
            jax.ShapeDtypeStruct((micro * HEADS, count, count), F32),
        ],
        cost_estimate=pl.CostEstimate(
            flops=4 * micro * HEADS * count * count * HEAD_DIM,
            bytes_accessed=micro * HEADS * count * count * 6,
            transcendentals=micro * HEADS * count * count,
        ),
        name="attend",
    )(projected, ids.reshape(micro * count, 1), ids.reshape(micro, 1, count))


def attend_back_kernel(proj_ref, prob_ref, datt_ref, dproj_ref, inner_ref):
    width = HEADS * HEAD_DIM
    keys = proj_ref[:, width : width + HEAD_DIM]
    values = proj_ref[:, width + HEAD_DIM :]
    grad_keys = None
    grad_values = None
    dot_total = 0.0
    for head in range(HEADS):
        part = slice(head * HEAD_DIM, (head + 1) * HEAD_DIM)
        probs = prob_ref[head]
        queries = proj_ref[:, part]
        d_att = datt_ref[:, part]
        d_probs = contract(d_att, values, 1, 1)
        row_inner = jnp.sum(d_probs * probs, axis=1, keepdims=True)
        d_scores = (probs * (d_probs - row_inner) * HEAD_DIM ** (-0.5)).astype(BF16)
        grad_q = contract(d_scores, keys, 1, 0).astype(BF16)
        dproj_ref[:, part] = grad_q
        dot_total = dot_total + grad_q.astype(F32) * queries.astype(F32)
        add_k = contract(d_scores, queries, 0, 0)
        add_v = contract(probs.astype(BF16), d_att, 0, 0)
        grad_keys = add_k if grad_keys is None else grad_keys + add_k
        grad_values = add_v if grad_values is None else grad_values + add_v
    grad_keys = grad_keys.astype(BF16)
    grad_values = grad_values.astype(BF16)
    dproj_ref[:, width : width + HEAD_DIM] = grad_keys
    dproj_ref[:, width + HEAD_DIM :] = grad_values
    dot_total = dot_total + grad_keys.astype(F32) * keys.astype(F32)
    dot_total = dot_total + grad_values.astype(F32) * values.astype(F32)
    inner_ref[...] = jnp.sum(dot_total, axis=1, keepdims=True)


def attend_back(projected, probs, d_att):
    total, width = projected.shape
    count = probs.shape[1]
    micro = total // count
    att_width = HEADS * HEAD_DIM
    return pl.pallas_call(
        attend_back_kernel,
        grid=(micro,),
        in_specs=[
            pl.BlockSpec((count, width), lambda m: (m, 0)),
            pl.BlockSpec((HEADS, count, count), lambda m: (m, 0, 0)),
            pl.BlockSpec((count, att_width), lambda m: (m, 0)),
        ],
        out_specs=[
            pl.BlockSpec((count, width), lambda m: (m, 0)),
            pl.BlockSpec((count, 1), lambda m: (m, 0)),
        ],
        out_shape=[
            jax.ShapeDtypeStruct((total, width), BF16),
            jax.ShapeDtypeStruct((total, 1), F32),
        ],
        cost_estimate=pl.CostEstimate(
            flops=8 * micro * HEADS * count * count * HEAD_DIM,
            bytes_accessed=micro * HEADS * count * count * 6,
            transcendentals=0,
        ),
        name="attend_back",
    )(projected, probs, d_att)


def normalize(tokens, gain_row):
    wide = tokens.astype(F32)
    inv_rms = lax.rsqrt(jnp.mean(wide * wide, axis=1, keepdims=True) + 1e-05)
    return inv_rms, (wide * inv_rms * gain_row).astype(BF16)


def body(
    x_forward,
    seg_forward,
    x_saved,
    x_earlier,
    cotangent,
    seg_backward,
    gain,
    qkv,
    proj,
    sum_gain,
    sum_qkv,
    sum_proj,
):
    x_next = shifted(x_earlier, "blk", -1)
    ids_next_b = shifted(seg_backward, "blk", -1)
    ids_next_f = shifted(seg_forward, "blk", -1)
    qkv_all = lax.all_gather(qkv[0], "fsdp", axis=0, tiled=True)
    gain_all = lax.all_gather(gain, "fsdp", axis=1, tiled=True).astype(F32)
    proj_all = lax.all_gather(proj[0], "fsdp", axis=1, tiled=True)

    features = x_saved.shape[1]
    inv_one, normed_one = normalize(x_saved, gain_all)
    inv_two, normed_two = normalize(x_next, gain_all)
    inv_fwd, normed_fwd = normalize(x_forward, gain_all)

    def project(normed):
        return jnp.dot(normed, qkv_all, preferred_element_type=F32).astype(BF16)

    proj_one = project(normed_one)
    att_one, probs_one = attend(proj_one, seg_backward)
    proj_fwd = project(normed_fwd)
    att_fwd, unused = attend(proj_fwd, seg_forward)
    proj_two = project(normed_two)
    att_two, probs_two = attend(proj_two, ids_next_b)

    d_att = contract(cotangent, proj_all, 1, 1).astype(BF16)
    d_proj_one, inner = attend_back(proj_one, probs_one, d_att)
    d_normed = contract(d_proj_one, qkv_all, 1, 1)
    d_hidden = (
        cotangent.astype(F32)
        + inv_one * gain_all * d_normed
        - x_saved.astype(F32) * (inv_one * inv_one * inner / features)
    ).astype(BF16)
    upstream = shifted(d_hidden, "blk", -1)

    hidden = (
        x_forward.astype(F32) + jnp.dot(att_fwd, proj_all, preferred_element_type=F32)
    ).astype(BF16)
    hidden_next = shifted(hidden, "blk", -1)

    d_att_two = contract(upstream, proj_all, 1, 1).astype(BF16)
    grad_proj = contract(
        jnp.concatenate([att_one, att_two], axis=0),
        jnp.concatenate([cotangent, upstream], axis=0),
        0,
        0,
    ).astype(BF16)
    reduced_proj = lax.psum_scatter(grad_proj, "fsdp", scatter_dimension=1, tiled=True)
    d_proj_two, unused = attend_back(proj_two, probs_two, d_att_two)
    grad_qkv = contract(
        jnp.concatenate([normed_one, normed_two], axis=0),
        jnp.concatenate([d_proj_one, d_proj_two], axis=0),
        0,
        0,
    ).astype(BF16)
    reduced_qkv = lax.psum_scatter(grad_qkv, "fsdp", scatter_dimension=0, tiled=True)

    inv_last, normed_last = normalize(hidden_next, gain_all)
    proj_last = project(normed_last)
    att_last, unused = attend(proj_last, ids_next_f)
    result = (
        hidden_next.astype(F32) + jnp.dot(att_last, proj_all, preferred_element_type=F32)
    ).astype(BF16)
    result = shifted(result, "blk", 1)

    new_proj = shifted((sum_proj[0] + reduced_proj.astype(F32)).astype(BF16), "blk", 1)
    wide_qkv = reduced_qkv.astype(F32)
    grad_gain = jnp.sum(wide_qkv * qkv[0].astype(F32), axis=1)[None] / gain.astype(F32)
    new_gain = shifted(sum_gain + grad_gain, "blk", 1)
    new_qkv = shifted((sum_qkv[0] + wide_qkv).astype(BF16), "blk", 1)
    return (result, new_gain, new_qkv.astype(F32)[None], new_proj.astype(F32)[None])


def solution(mesh):
    rows = P(("blk", "fsdp"), None)
    weights = (P("blk", "fsdp"), P("blk", "fsdp", None), P("blk", None, "fsdp"))
    return jax.shard_map(
        body,
        mesh=mesh,
        in_specs=(rows,) * 6 + weights + weights,
        out_specs=(rows,) + weights,
        check_vma=False,
    )
```
